128 devices in a mesh: group: 4 (over x), tile: 32 (over z, y, core).
Axes of the slice: x: 4, y: 4, z: 4, core: 2. Of those that a mesh axis runs over, the one named last changes fastest.
Arguments:
- frames: bfloat16 [12, 8, 128, 96, 256], P('group', None, 'tile'), may hold values from -6 to 6
- packing: int32 [12, 4], replicated, as said below
- w_space: bfloat16 [3, 3, 96, 96], replicated, may hold values from -0.21875 to 0.21875
- w_time: bfloat16 [3, 96, 96], replicated, may hold values from -0.375 to 0.375
- gain_one: float32 [96], replicated, may hold values from 0.1 to 1.9
- gain_two: float32 [96], replicated, may hold values from 0.1 to 1.9
Outputs:
- output: bfloat16 [12, 8, 128, 96, 256], P('group', None, 'tile')
The draws below stay inside these ranges and needn't reach their ends.
Inputs may be any that keep to these rules, and one draw needn't show every extreme that they name: `packing`: column 0 is 1 where the slot's span continues a clip and 0 for a clip's first span, whose other source fields are not read. `packing`: a span with a successor has 8 valid frames, so every preceding span is full; the slots of one device have their preceding spans on distinct devices.
All inputs are finite; a program needn't handle non-finite values.
Results may differ from the reference program's by a relative error of at most 0.004.
Values may be sent and summed in bfloat16 or wider, within the bound.
No kernel may reach another device: no remote copies, remote signals or barrier semaphores. Data moves between devices by JAX's collectives and lax.ppermute only.
A program may use at most 192 MiB of HBM per device.

```python
import jax
import jax.numpy as jnp
from jax import lax

CHANNELS = 96
FRAMES = 8
SLOTS = 3
COLS = 256
SLOTS_ALL = 12
ROWS = 128


def draw_packing(key, part):
    span_count = SLOTS_ALL // SLOTS
    key_perm, key_head, key_count = jax.random.split(jax.random.fold_in(key, 7), 3)
    orders = jax.vmap(lambda sub: jax.random.permutation(sub, SLOTS))(jax.random.split(key_perm, span_count)).astype(jnp.int32)
    global_ids = jnp.arange(SLOTS_ALL, dtype=jnp.int32)
    device_of = global_ids // SLOTS
    slot_of = global_ids % SLOTS
    src_device = (device_of - 1 - slot_of) % span_count
    src_slot = orders[src_device, slot_of]
    previous = (src_device * SLOTS + src_slot).astype(jnp.int32)

    def lowest_step(turn_index, state):
        current, lowest = state
        current = previous[current]
        return (current, jnp.minimum(lowest, current))
    _, lowest = lax.fori_loop(0, SLOTS_ALL, lowest_step, (global_ids, global_ids))
    heads = (jax.random.randint(key_head, (SLOTS_ALL,), 0, 3) == 0) | (lowest == global_ids)
    successor = jnp.zeros((SLOTS_ALL,), jnp.int32).at[previous].set(global_ids)
    is_last = heads[successor]
    drawn = jax.random.randint(key_count, (SLOTS_ALL,), 1, FRAMES + 1)
    valid = jnp.where(is_last & (global_ids != 0), drawn, FRAMES)
    continues = jnp.where(heads, 0, 1).astype(jnp.int32)
    return jnp.stack([continues, valid, src_device, src_slot], axis=1).astype(jnp.int32)


def shard_levels(rng, shape, shards, smallest, top_value):
    level = 1.0
    for dim, shards_of in shards:
        steps = jax.random.uniform(jax.random.fold_in(jax.random.fold_in(rng, 6), dim), (shards_of,), jnp.float32, smallest / len(shards), top_value / len(shards))
        level = level * jnp.repeat(jnp.exp(steps), shape[dim] // shards_of).reshape((-1,) + (1,) * (len(shape) - 1 - dim))
    return level


def gaussian(key, extent, spread, limit, cuts=(), held_as=jnp.bfloat16):
    values = jax.random.normal(key, extent, jnp.float32) * spread
    if len(cuts) > 0:
        values = shard_levels(key, extent, cuts, -0.22, 0.18) * values
    return jnp.clip(values, min=-limit, max=limit).astype(held_as)


def setup_inputs(seed: int = 0) -> dict:
    key_list = jax.random.split(jax.random.key(seed), 7)
    return {
        "frames": gaussian(key_list[0], (SLOTS_ALL, FRAMES, ROWS, CHANNELS, COLS), 1.0, 6.0, ((0, 4), (2, 32))),
        "packing": draw_packing(jax.random.fold_in(key_list[6], 71), 0),
        "w_space": gaussian(key_list[2], (3, 3, CHANNELS, CHANNELS), (9 * CHANNELS) ** -0.5, 0.21875),
        "w_time": gaussian(key_list[3], (3, CHANNELS, CHANNELS), (3 * CHANNELS) ** -0.5, 0.375),
        "gain_one": jnp.clip(1.0 + 0.18 * jax.random.normal(key_list[4], (CHANNELS,), jnp.float32), 0.1, 1.9),
        "gain_two": jnp.clip(1.0 + 0.18 * jax.random.normal(key_list[5], (CHANNELS,), jnp.float32), 0.1, 1.9),
    }


def norm_act(values, gain_vec):
    meansq = lax.optimization_barrier(jnp.mean(values * values, axis=-2, keepdims=True))
    return jax.nn.silu(values * lax.rsqrt(meansq + 1e-06) * gain_vec[:, None])

def reference(frames, packing, w_space, w_time, gain_one, gain_two):
    space_f = w_space.astype(jnp.float32)
    time_f = w_time.astype(jnp.float32)

    def branch(slot_frames):
        hidden = norm_act(slot_frames.astype(jnp.float32), gain_one).astype(jnp.bfloat16)
        padded = jnp.pad(hidden.astype(jnp.float32), ((0, 0), (1, 1), (0, 0), (1, 1)))
        summed = jnp.zeros(slot_frames.shape, jnp.float32)
        for tap_row in range(3):
            for tap_col in range(3):
                window = padded[:, tap_row:tap_row + ROWS, :, tap_col:tap_col + COLS]
                summed = summed + jnp.einsum('oi,fyix->fyox', space_f[tap_row, tap_col], window, precision=lax.Precision.HIGHEST)
        return norm_act(summed, gain_two).astype(jnp.bfloat16)
    act = lax.map(branch, frames)
    tails = act[:, FRAMES - 2:]
    source = (packing[:, 2] * SLOTS + packing[:, 3]).astype(jnp.int32)
    has_prev = packing[:, 0] > 0
    cache = jnp.where(has_prev[:, None, None, None, None], tails[source], jnp.zeros_like(tails))

    def finish(items):
        slot_frames, slot_act, slot_cache, valid = items
        extended = jnp.concatenate([slot_cache, slot_act], axis=0).astype(jnp.float32)
        temporal = jnp.zeros(slot_frames.shape, jnp.float32)
        for tap in range(3):
            temporal = temporal + jnp.einsum('oi,fyix->fyox', time_f[tap], extended[tap:tap + FRAMES], precision=lax.Precision.HIGHEST)
        keep = jnp.arange(FRAMES) < valid
        result = jnp.where(keep[:, None, None, None], slot_frames.astype(jnp.float32) + temporal, 0.0)
        return result.astype(jnp.bfloat16)
    return lax.map(finish, (frames, act, cache, packing[:, 1]))
```

```python
import functools

import jax
import jax.numpy as jnp
from jax import lax
from jax.experimental import pallas as pl
from jax.experimental.pallas import tpu as pltpu
from jax.sharding import PartitionSpec as P

F32 = jnp.float32
BF16 = jnp.bfloat16
TAIL = 2


def silu_norm(values, half_gain):
    meansq = jnp.mean(values * values, axis=0, keepdims=True)
    half = values * lax.rsqrt(meansq + 1e-06) * half_gain
    return (half + half * jnp.tanh(half)).astype(BF16)


def put_row(scr, row, chan, hidden):
    cols = hidden.shape[1]
    lane = lax.broadcasted_iota(jnp.int32, hidden.shape, 1)
    zero = jnp.zeros_like(hidden)
    left = jnp.where(lane == 0, zero, pltpu.roll(hidden, 1, 1))
    right = jnp.where(lane == cols - 1, zero, pltpu.roll(hidden, cols - 1, 1))
    base = row * (3 * chan)
    if not isinstance(base, int):
        base = pl.multiple_of(base, 32)
    scr[pl.ds(base, chan), :] = left
    scr[pl.ds(base + chan, chan), :] = hidden
    scr[pl.ds(base + 2 * chan, chan), :] = right


def act_rows(rows, frame, pair, out, wcat, gain_one, gain_two, scr, odd):
    chan = gain_one.shape[0]
    half_one = gain_one[...]
    put_row(scr, (1 - odd) * (rows + 1), chan, silu_norm(pair(), half_one))
    put_row(scr, odd * (rows + 1), chan, silu_norm(out(), half_one))
    for y in range(rows):
        put_row(scr, y + 1, chan, silu_norm(frame(y), half_one))
    half_two = gain_two[...]
    result = []
    for y in range(rows):
        window = scr[y * 3 * chan : (y + 3) * 3 * chan, :]
        spatial = jnp.dot(wcat[...], window, preferred_element_type=F32)
        result.append(silu_norm(spatial, half_two))
    return result


def tail_kernel(slots, groups, pack, ids, frame, pair, out, wcat, g1, g2, tails, *rest):
    sends, scr = rest[:-1], rest[-1]
    n, j = pl.program_id(0), pl.program_id(1)
    me, odd = ids[0], ids[1]
    rows = frame.shape[2]
    acts = act_rows(
        rows,
        lambda y: frame[0, 0, y].astype(F32),
        lambda: pair[0, 0].astype(F32),
        lambda: out[0, 0].astype(F32),
        wcat, g1, g2, scr, odd,
    )
    for y in range(rows):
        tails[0, 0, y] = acts[y]
    for s in range(1, groups):
        dst = lax.rem(me + s, groups)
        wanted = jnp.int32(-1)
        for k in range(slots):
            g = dst * slots + k
            hit = (pack[g, 0] > 0) & (pack[g, 2] == me)
            wanted = jnp.where(hit, pack[g, 3], wanted)

        @pl.when(wanted == n)
        def _():
            sends[s - 1][j] = tails[0, 0]


def main_kernel(slots, pack, ids, frame, pair, out, tails, wcat, wrot, g1, g2, result, heads, scr, ring):
    n, j = pl.program_id(0), pl.program_id(1)
    me, odd = ids[0], ids[1]
    frames, rows = pl.num_programs(1), frame.shape[2]
    chan = g1.shape[0]
    place = lax.rem(j, 3)
    base = pl.multiple_of(place * chan, 32)

    @pl.when(j < frames - TAIL)
    def _():
        acts = act_rows(
            rows,
            lambda y: frame[0, 0, y].astype(F32),
            lambda: pair[0, 0].astype(F32),
            lambda: out[0, 0].astype(F32),
            wcat, g1, g2, scr, odd,
        )
        for y in range(rows):
            ring[y, pl.ds(base, chan), :] = acts[y]

    @pl.when(j < TAIL)
    def _():
        for y in range(rows):
            heads[0, j, y] = ring[y, pl.ds(base, chan), :]

    @pl.when(j >= frames - TAIL)
    def _():
        for y in range(rows):
            ring[y, pl.ds(base, chan), :] = tails[0, 0, y]

    @pl.when(j >= TAIL)
    def _():
        keep = j < pack[me * slots + n, 1]
        for y in range(rows):
            temporal = jnp.dot(wrot[place], ring[y], preferred_element_type=F32)
            total = frame[0, 0, y].astype(F32) + temporal
            result[0, 0, y] = jnp.where(keep, total, 0.0).astype(BF16)


def head_kernel(slots, groups, pack, ids, frame, heads, tails, wtime, *rest):
    recvs, result, scr = rest[: groups - 1], rest[-2], rest[-1]
    n = pl.program_id(0)
    me = ids[0]
    rows, chan = frame.shape[2], frame.shape[3]
    g = me * slots + n
    has_prev, source = pack[g, 0] > 0, pack[g, 2]
    for y in range(rows):
        for f in range(TAIL):
            scr[y, (TAIL + f) * chan : (TAIL + f + 1) * chan, :] = heads[0, f, y]

    def put(load):
        for y in range(rows):
            for f in range(TAIL):
                scr[y, f * chan : (f + 1) * chan, :] = load(f, y)

    @pl.when(jnp.logical_not(has_prev))
    def _():
        put(lambda f, y: jnp.zeros(scr.shape[-1:], BF16) + jnp.zeros((chan, 1), BF16))

    @pl.when(has_prev & (source == me))
    def _():
        put(lambda f, y: tails[0, f, y])

    for s in range(1, groups):
        @pl.when(has_prev & (source == lax.rem(me + groups - s, groups)))
        def _():
            put(lambda f, y: recvs[s - 1][f, y])

    for f in range(TAIL):
        keep = f < pack[g, 1]
        for y in range(rows):
            window = scr[y, f * chan : (f + 3) * chan, :]
            temporal = jnp.dot(wtime[...], window, preferred_element_type=F32)
            total = frame[0, f, y].astype(F32) + temporal
            result[0, f, y] = jnp.where(keep, total, 0.0).astype(BF16)


def body(frames, packing, w_space, w_time, gain_one, gain_two):
    slots, count, rows, chan, cols = frames.shape
    groups, tiles = lax.axis_size("group"), lax.axis_size("tile")
    me = lax.axis_index("group").astype(jnp.int32)
    odd = lax.rem(lax.axis_index("tile"), 2).astype(jnp.int32)
    ids = jnp.stack([me, odd])
    lead = count - TAIL

    pairs = [(i, i ^ 1) for i in range(tiles)]
    outs = [(i, i + 1 if i % 2 else i - 1) for i in range(1, tiles - 1)]
    pair_row = (1 - odd) * (rows - 1)
    out_row = odd * (rows - 1)

    def edge(row, first, size):
        sizes = (slots, size, 1, chan, cols)
        return lax.dynamic_slice(frames, (0, first, row, 0, 0), sizes).reshape(slots, size, chan, cols)

    tail_pair = lax.ppermute(edge(pair_row, lead, TAIL), "tile", pairs)
    tail_out = lax.ppermute(edge(out_row, lead, TAIL), "tile", outs)
    lead_pair = lax.ppermute(edge(pair_row, 0, lead), "tile", pairs)
    lead_out = lax.ppermute(edge(out_row, 0, lead), "tile", outs)

    wcat = w_space.transpose(2, 0, 1, 3).reshape(chan, 9 * chan)
    wtime = w_time.transpose(1, 0, 2).reshape(chan, 3 * chan)
    wrot = jnp.stack(
        [
            jnp.concatenate([w_time[(slot - r + 2) % 3] for slot in range(3)], axis=1)
            for r in range(3)
        ]
    )
    half_one = jnp.broadcast_to((0.5 * gain_one)[:, None], (chan, cols))
    half_two = jnp.broadcast_to((0.5 * gain_two)[:, None], (chan, cols))

    row_block = (1, 1, rows, chan, cols)
    halo_block = (1, 1, chan, cols)
    whole = lambda shape: pl.BlockSpec(shape, lambda *_: (0,) * len(shape))
    frame_flops = 2 * rows * cols * chan * chan
    frame_bytes = 2 * rows * cols * chan

    tails, *sends = pl.pallas_call(
        functools.partial(tail_kernel, slots, groups),
        out_shape=[jax.ShapeDtypeStruct((slots, TAIL, rows, chan, cols), BF16)]
        + [jax.ShapeDtypeStruct((TAIL, rows, chan, cols), BF16)] * (groups - 1),
        grid_spec=pltpu.PrefetchScalarGridSpec(
            num_scalar_prefetch=2,
            grid=(slots, TAIL),
            in_specs=[
                pl.BlockSpec(row_block, lambda n, j, *_: (n, lead + j, 0, 0, 0)),
                pl.BlockSpec(halo_block, lambda n, j, *_: (n, j, 0, 0)),
                pl.BlockSpec(halo_block, lambda n, j, *_: (n, j, 0, 0)),
                whole((chan, 9 * chan)),
                whole((chan, cols)),
                whole((chan, cols)),
            ],
            out_specs=[pl.BlockSpec(row_block, lambda n, j, *_: (n, j, 0, 0, 0))]
            + [whole((TAIL, rows, chan, cols))] * (groups - 1),
            scratch_shapes=[pltpu.VMEM(((rows + 2) * 3 * chan, cols), BF16)],
        ),
        name="tails",
        cost_estimate=pl.CostEstimate(
            flops=slots * TAIL * 9 * frame_flops,
            bytes_accessed=slots * TAIL * 3 * frame_bytes,
            transcendentals=slots * TAIL * rows * cols * chan * 2,
        ),
    )(packing, ids, frames, tail_pair, tail_out, wcat, half_one, half_two)

    recvs = [
        lax.ppermute(sends[s - 1], "group", [(i, (i + s) % groups) for i in range(groups)])
        for s in range(1, groups)
    ]

    result, heads = pl.pallas_call(
        functools.partial(main_kernel, slots),
        out_shape=[
            jax.ShapeDtypeStruct(frames.shape, BF16),
            jax.ShapeDtypeStruct((slots, TAIL, rows, chan, cols), BF16),
        ],
        grid_spec=pltpu.PrefetchScalarGridSpec(
            num_scalar_prefetch=2,
            grid=(slots, count),
            in_specs=[
                pl.BlockSpec(row_block, lambda n, j, *_: (n, j, 0, 0, 0)),
                pl.BlockSpec(halo_block, lambda n, j, *_: (n, jnp.minimum(j, lead - 1), 0, 0)),
                pl.BlockSpec(halo_block, lambda n, j, *_: (n, jnp.minimum(j, lead - 1), 0, 0)),
                pl.BlockSpec(row_block, lambda n, j, *_: (n, jnp.maximum(j - lead, 0), 0, 0, 0)),
                whole((chan, 9 * chan)),
                whole((3, chan, 3 * chan)),
                whole((chan, cols)),
                whole((chan, cols)),
            ],
            out_specs=[
                pl.BlockSpec(row_block, lambda n, j, *_: (n, jnp.maximum(j, TAIL), 0, 0, 0)),
                pl.BlockSpec((1, TAIL, rows, chan, cols), lambda n, j, *_: (n, 0, 0, 0, 0)),
            ],
            scratch_shapes=[
                pltpu.VMEM(((rows + 2) * 3 * chan, cols), BF16),
                pltpu.VMEM((rows, 3 * chan, cols), BF16),
            ],
        ),
        name="lead",
        cost_estimate=pl.CostEstimate(
            flops=slots * lead * 12 * frame_flops,
            bytes_accessed=slots * count * 2 * frame_bytes,
            transcendentals=slots * lead * rows * cols * chan * 2,
        ),
    )(packing, ids, frames, lead_pair, lead_out, tails, wcat, wrot, half_one, half_two)

    head_block = (1, TAIL, rows, chan, cols)

    def local_tail(n, pack, ids):
        return (jnp.clip(pack[ids[0] * slots + n, 3], 0, slots - 1), 0, 0, 0, 0)

    return pl.pallas_call(
        functools.partial(head_kernel_entry, slots, groups),
        out_shape=jax.ShapeDtypeStruct(frames.shape, BF16),
        grid_spec=pltpu.PrefetchScalarGridSpec(
            num_scalar_prefetch=2,
            grid=(slots,),
            in_specs=[
                pl.BlockSpec(head_block, lambda n, *_: (n, 0, 0, 0, 0)),
                pl.BlockSpec(head_block, lambda n, *_: (n, 0, 0, 0, 0)),
                pl.BlockSpec(head_block, local_tail),
                whole((chan, 3 * chan)),
            ]
            + [whole((TAIL, rows, chan, cols))] * (groups - 1)
            + [pl.BlockSpec(memory_space=pl.ANY)],
            out_specs=pl.BlockSpec(head_block, lambda n, *_: (n, 0, 0, 0, 0)),
            scratch_shapes=[pltpu.VMEM((rows, 2 * TAIL * chan, cols), BF16)],
        ),
        input_output_aliases={6 + groups - 1: 0},
        name="heads",
        cost_estimate=pl.CostEstimate(
            flops=slots * TAIL * 3 * frame_flops,
            bytes_accessed=slots * TAIL * 4 * frame_bytes,
            transcendentals=0,
        ),
    )(packing, ids, frames, heads, tails, wtime, *recvs, result)


def head_kernel_entry(slots, groups, pack, ids, frame, heads, tails, wtime, *rest):
    recvs, result, scr = rest[: groups - 1], rest[-2], rest[-1]
    head_kernel(slots, groups, pack, ids, frame, heads, tails, wtime, *recvs, result, scr)


def solution(mesh):
    in_specs = (P("group", None, "tile", None, None), P(), P(), P(), P(), P())
    out_specs = P("group", None, "tile", None, None)
    return jax.shard_map(body, mesh=mesh, in_specs=in_specs, out_specs=out_specs, check_vma=False)
```
